32 devices in a mesh: end: 2 (over x), slab: 16 (over z, y, core).
Axes of the slice: x: 2, y: 2, z: 4, core: 2. Of those that a mesh axis runs over, the one named last changes fastest.
Arguments:
- w_field: float32 [128, 128, 256], P('slab'), may hold values from -4 to 4
- psi_init: float32 [128, 128, 256], P('slab'), may hold values from -3 to 3
- start_field: float32 [2, 128, 128, 256], P('end', 'slab'), may hold values from 0.25 to 8, as said below
- charges: int32 [5], replicated, may hold values from -1 to 1
Outputs:
- density: float32 [128, 128, 256], P('slab', 'end')
- potential: float32 [128, 128, 256], P('slab', 'end')
The draws below stay inside these ranges and needn't reach their ends.
Inputs may be any that keep to these rules, and one draw needn't show every extreme that they name: `start_field`: positive entries.
All inputs are finite; a program needn't handle non-finite values.
Results may differ from the reference program's by a relative error of at most 0.0003.
The reference program's roundings to bfloat16 on the way count: a program that leaves them out, or rounds other values in their place, can miss the bound.
Values may be sent and summed in bfloat16 or wider, within the bound.
A program may use at most 64 MiB of HBM per device.

```python
import jax
import jax.numpy as jnp
from jax import lax

NY = 128
NZ = 256
NS = 4
SWEEPS = 2
NX = 128


def draw_start_field(key, part):
    position = jnp.arange(NX, dtype=jnp.float32) / (NX - 1)
    base = jax.random.uniform(key, (2, NX, NY, NZ), jnp.float32, 0.5, 1.5)
    ramp = 1.0 + 2.0 * position
    return base * ramp[None, :, None, None]


def set_ends(drawn, key, low, largest):
    longest = drawn.shape.index(max(drawn.shape))
    spots = []
    for shift in (0, 1):
        where = [jax.random.randint(jax.random.fold_in(key, axis), (), 0, length) for axis, length in enumerate(drawn.shape)]
        where[longest] = (where[longest] + shift) % drawn.shape[longest]
        spots.append(tuple(where))
    return drawn.at[spots[0]].set(low).at[spots[1]].set(largest)


def levels(own_key, shape, split, least, top_value):
    factor_of = 1.0
    for dim, parts in split:
        heights = jax.random.uniform(jax.random.fold_in(jax.random.fold_in(own_key, 6), dim), (parts,), jnp.float32, least / len(split), top_value / len(split))
        factor_of = factor_of * jnp.repeat(jnp.exp(heights), shape[dim] // parts).reshape((-1,) + (1,) * (len(shape) - 1 - dim))
    return factor_of


def noise(rng, dims, deviation, bound, pieces=(), kind=jnp.bfloat16):
    factor_of = levels(rng, dims, pieces, -0.22, 0.18) if pieces else 1.0
    entries = jax.random.normal(rng, dims, jnp.float32) * deviation * factor_of
    return jnp.minimum(jnp.maximum(entries, -bound), bound).astype(kind)


def setup_inputs(seed: int = 0) -> dict:
    splits = jax.random.split(jax.random.key(seed), 5)
    w_field = noise(splits[0], (NX, NY, NZ), 1.0, 4.0, ((0, 16),), jnp.float32)
    psi_init = noise(splits[1], (NX, NY, NZ), 0.5, 3.0, ((0, 16),), jnp.float32)
    start_field = draw_start_field(jax.random.fold_in(splits[4], 71), 0)
    charges = set_ends(jax.random.randint(splits[3], (NS + 1,), -1, 2), jax.random.fold_in(splits[3], 1), -1, 1).astype(jnp.int32)
    return dict(w_field=w_field, psi_init=psi_init, start_field=start_field, charges=charges)


mobility = 0.15
screening = 1.0
crowding = 0.5


def neighbour_sum(field):
    total = jnp.roll(field, 1, 0) + jnp.roll(field, -1, 0)
    total = total + jnp.roll(field, 1, 1) + jnp.roll(field, -1, 1)
    return total + jnp.roll(field, 1, 2) + jnp.roll(field, -1, 2)


def ion_charge(value):
    return screening * jnp.sinh(value) / (1.0 + crowding * (jnp.cosh(value) - 1.0))


def reference(w_field, psi_init, start_field, charges):
    delta = 1.0 / NS
    valence = charges.astype(jnp.float32)

    def advance(field, contour):
        factor = jnp.exp(-0.5 * delta * (w_field + 0.5 * (valence[contour] + valence[contour + 1]) * psi_init))
        scaled = factor * field
        return factor * (scaled + mobility * (neighbour_sum(scaled) - 6.0 * scaled))

    def rounded(field):
        return lax.optimization_barrier(field.astype(jnp.bfloat16)).astype(jnp.float32)

    forward = [start_field[0]]
    for contour in range(NS):
        forward.append(advance(forward[-1], contour))
    conjugate = start_field[1]
    phi_raw = jnp.zeros(w_field.shape, jnp.float32)
    rho_raw = jnp.zeros(w_field.shape, jnp.float32)
    for contour in range(NS, -1, -1):
        if contour < NS:
            conjugate = advance(conjugate, contour)
        product = rounded(forward[contour]) * rounded(conjugate)
        weight = delta * (0.5 if contour in (0, NS) else 1.0)
        phi_raw = phi_raw + weight * product
        rho_raw = rho_raw + (weight * valence[contour]) * product
    total = jnp.mean(phi_raw)
    density = phi_raw / total
    charge = rho_raw / total
    potential = psi_init
    for sweep in range(SWEEPS):
        potential = (neighbour_sum(potential) + charge - ion_charge(potential) + screening * potential) / (6.0 + screening)
    return density, potential
```

```python
import functools

import jax
import jax.numpy as jnp
from jax import lax
from jax.experimental import pallas as pl
from jax.experimental.pallas import tpu as pltpu
from jax.sharding import PartitionSpec as P

NS = 4
PAD = 8
mobility = 0.15
screening = 1.0
OWN, FOREIGN = 0, 1
MESH = pl.DeviceIdType.MESH


def kernel(ends, slabs, charges_ref, w_hbm, psi_hbm, start_hbm, density_ref, potential_ref,
           w_v, psi_v, start_v, factor, u, rounded, phi, rho, base, relaxed, sums,
           local_sem, field_send, field_recv, psi_send, psi_recv, halo_send, halo_recv,
           rho_send, rho_recv, sum_send, sum_recv):
    side, slab = lax.axis_index("end"), lax.axis_index("slab")
    other = lax.rem(side + 1, ends)
    left = (side, lax.rem(slab + slabs - 1, slabs))
    right = (side, lax.rem(slab + 1, slabs))
    partner = (other, slab)
    layers, rows = w_hbm.shape[0], w_hbm.shape[1]
    half = rows // ends
    devices = ends * slabs
    flat = side * slabs + slab
    delta = 1.0 / NS

    def device(step):
        target = lax.rem(flat + step, devices)
        return (target // slabs, lax.rem(target, slabs))

    barrier = pltpu.get_barrier_semaphore()

    def greet(step, carry):
        pl.semaphore_signal(barrier, inc=1, device_id=device(step), device_id_type=MESH)
        return carry

    lax.fori_loop(1, devices, greet, 0)

    def pieces(which):
        first = which * half
        return (
            (pl.multiple_of(first, 8), PAD, half),
            (pl.multiple_of(lax.rem(first + rows - PAD, rows), 8), 0, PAD),
            (pl.multiple_of(lax.rem(first + half, rows), 8), PAD + half, PAD),
        )

    mine, theirs = pieces(side), pieces(other)
    local = []
    for k, (source, target, first) in enumerate(
        ((w_hbm, w_v, 0), (psi_hbm, psi_v, 2), (start_hbm.at[0], start_v.at[OWN], 0))
    ):
        for n, (begin, at, count) in enumerate(mine):
            local.append(
                pltpu.make_async_copy(
                    source.at[:, pl.ds(begin, count)],
                    target.at[pl.ds(first, layers), pl.ds(at, count)],
                    local_sem.at[k, n],
                )
            )
    for copy in local:
        copy.start()
    for copy in local:
        copy.wait()

    q = [charges_ref[side * (NS - 2 * t) + t].astype(jnp.float32) for t in range(NS + 1)]
    pair = [0.5 * (q[k] + q[k + 1]) for k in range(NS)]

    def make_factor(x, carry):
        w, psi = w_v[x], psi_v[x + 2]
        for k in range(NS):
            factor[k, x] = jnp.exp(-0.5 * delta * (w + pair[k] * psi))
        return carry

    def index(chain, t):
        return t if chain == OWN else NS - 1 - t

    def begin_chain(chain, x):
        value = start_v[chain, x]
        rounded[chain, 0, x] = value.astype(jnp.bfloat16).astype(jnp.float32)
        u[chain, 0, x + 1] = factor[index(chain, 0), x] * value

    def around(value, axis):
        return pltpu.roll(value, 1, axis) + pltpu.roll(value, value.shape[axis] - 1, axis)

    def advanced(chain, t, x):
        center = u[chain, t, x + 1]
        total = u[chain, t, x] + u[chain, t, x + 2] + around(center, 0) + around(center, 1)
        return factor[index(chain, t), x] * (center + mobility * (total - 6.0 * center))

    def advance(chain, t, x):
        value = advanced(chain, t, x)
        rounded[chain, t + 1, x] = value.astype(jnp.bfloat16).astype(jnp.float32)
        if t + 1 < NS:
            u[chain, t + 1, x + 1] = factor[index(chain, t + 1), x] * value

    def loop(low, high, step):
        def body(x, carry):
            step(x)
            return carry

        lax.fori_loop(low, high, body, 0)

    def both(step):
        step(0)
        step(layers - 1)

    def halo(chain, t):
        return (
            pltpu.make_async_remote_copy(
                u.at[chain, t, 1], u.at[chain, t, layers + 1],
                halo_send.at[chain, t, 0], halo_recv.at[chain, t, 0],
                device_id=left, device_id_type=MESH,
            ),
            pltpu.make_async_remote_copy(
                u.at[chain, t, layers], u.at[chain, t, 0],
                halo_send.at[chain, t, 1], halo_recv.at[chain, t, 1],
                device_id=right, device_id_type=MESH,
            ),
        )

    sent = []

    def send_halo(chain, t):
        for copy in halo(chain, t):
            copy.start()
            sent.append(copy)

    def wait_halo(chain, t):
        for copy in halo(chain, t):
            copy.wait_recv()

    groups = [(0, layers - 1), (1, layers - 2), (2, layers - 3), tuple(range(3, layers - 3))]
    order = [x for group in groups for x in group]

    def field(x):
        return [
            pltpu.make_async_remote_copy(
                start_hbm.at[0, x, pl.ds(begin, count)],
                start_v.at[FOREIGN, x, pl.ds(at, count)],
                field_send.at[x, n], field_recv.at[x, n],
                device_id=partner, device_id_type=MESH,
            )
            for n, (begin, at, count) in enumerate(theirs)
        ]

    def arrive(group):
        for x in groups[group]:
            for copy in field(x):
                copy.wait_recv()
        for x in groups[group]:
            begin_chain(FOREIGN, x)

    def psi_halo():
        copies = []
        for n, (begin, at, count) in enumerate(mine):
            copies.append(
                pltpu.make_async_remote_copy(
                    psi_hbm.at[pl.ds(0, 2), pl.ds(begin, count)],
                    psi_v.at[pl.ds(layers + 2, 2), pl.ds(at, count)],
                    psi_send.at[0, n], psi_recv.at[0, n],
                    device_id=left, device_id_type=MESH,
                )
            )
            copies.append(
                pltpu.make_async_remote_copy(
                    psi_hbm.at[pl.ds(layers - 2, 2), pl.ds(begin, count)],
                    psi_v.at[pl.ds(0, 2), pl.ds(at, count)],
                    psi_send.at[1, n], psi_recv.at[1, n],
                    device_id=right, device_id_type=MESH,
                )
            )
        return copies

    lax.fori_loop(0, layers, make_factor, 0)
    loop(0, layers, functools.partial(begin_chain, OWN))
    pl.semaphore_wait(barrier, devices - 1)

    for x in order:
        for copy in field(x):
            copy.start()
            sent.append(copy)
    send_halo(OWN, 0)
    psi_copies = psi_halo()
    for copy in psi_copies:
        copy.start()
        sent.append(copy)
    loop(1, layers - 1, functools.partial(advance, OWN, 0))

    arrive(0)
    send_halo(FOREIGN, 0)
    wait_halo(OWN, 0)
    both(functools.partial(advance, OWN, 0))
    send_halo(OWN, 1)
    loop(1, layers - 1, functools.partial(advance, OWN, 1))

    arrive(1)
    wait_halo(FOREIGN, 0)
    both(functools.partial(advance, FOREIGN, 0))
    send_halo(FOREIGN, 1)
    wait_halo(OWN, 1)
    both(functools.partial(advance, OWN, 1))
    send_halo(OWN, 2)
    loop(1, layers - 1, functools.partial(advance, OWN, 2))

    arrive(2)
    for x in (1, layers - 2):
        advance(FOREIGN, 0, x)
    wait_halo(FOREIGN, 1)
    both(functools.partial(advance, FOREIGN, 1))
    send_halo(FOREIGN, 2)
    wait_halo(OWN, 2)
    both(functools.partial(advance, OWN, 2))
    send_halo(OWN, 3)
    loop(1, layers - 1, functools.partial(advance, OWN, 3))

    arrive(3)
    loop(2, layers - 2, functools.partial(advance, FOREIGN, 0))
    loop(1, layers - 1, functools.partial(advance, FOREIGN, 1))
    wait_halo(FOREIGN, 2)
    both(functools.partial(advance, FOREIGN, 2))
    send_halo(FOREIGN, 3)
    loop(1, layers - 1, functools.partial(advance, FOREIGN, 2))
    wait_halo(OWN, 3)
    both(functools.partial(advance, OWN, 3))

    weights = [delta * (0.5 if t in (0, NS) else 1.0) for t in range(NS + 1)]
    charged = [weights[t] * q[t] for t in range(NS + 1)]

    def gather(x):
        phi_layer, rho_layer = 0.0, 0.0
        for t in range(1, NS + 1):
            product = rounded[OWN, t, x] * rounded[FOREIGN, NS - t, x]
            phi_layer = phi_layer + weights[t] * product
            rho_layer = rho_layer + charged[t] * product
        phi[x] = phi_layer
        rho[x + 1] = rho_layer

    def finish(x):
        value = advanced(FOREIGN, NS - 1, x).astype(jnp.bfloat16).astype(jnp.float32)
        product = rounded[OWN, 0, x] * value
        phi[x] += weights[0] * product
        rho[x + 1] += charged[0] * product

    loop(0, layers, gather)
    loop(1, layers - 1, finish)

    for copy in psi_copies:
        copy.wait_recv()

    def make_base(x):
        center = psi_v[x + 1]
        total = psi_v[x] + psi_v[x + 2] + around(center, 0) + around(center, 1)
        base[x] = total - ion_charge(center) + screening * center

    loop(0, layers + 2, make_base)

    wait_halo(FOREIGN, NS - 1)
    both(finish)
    rho_copies = (
        pltpu.make_async_remote_copy(
            rho.at[1], rho.at[layers + 1], rho_send.at[0], rho_recv.at[0],
            device_id=left, device_id_type=MESH,
        ),
        pltpu.make_async_remote_copy(
            rho.at[layers], rho.at[0], rho_send.at[1], rho_recv.at[1],
            device_id=right, device_id_type=MESH,
        ),
    )
    inner = pl.ds(PAD, half)

    def add(x, carry):
        return carry + phi[x, inner]

    partial = lax.fori_loop(1, layers, add, phi[0, inner])
    sums[0] = jnp.sum(
        sum(partial[:, k:k + 128] for k in range(0, partial.shape[1], 128)), axis=0, keepdims=True
    )

    def share(step, carry):
        pltpu.make_async_remote_copy(
            sums.at[0], sums.at[step], sum_send, sum_recv,
            device_id=device(step), device_id_type=MESH,
        ).start()
        return carry

    lax.fori_loop(1, devices, share, 0)
    for copy in rho_copies:
        copy.start()
        sent.append(copy)

    others = sums.at[pl.ds(1, devices - 1)]
    pltpu.make_async_copy(others, others, sum_recv).wait()
    cells = float(devices * layers * half * w_hbm.shape[2])
    inverse = cells / jnp.sum(sums[...])

    def relax_once(x):
        relaxed[x] = (base[x] + rho[x] * inverse) * (1.0 / (6.0 + screening))

    def first(x):
        density_ref[x] = phi[x, inner] * inverse
        relax_once(x + 1)

    loop(0, layers, first)

    def second(x):
        center = relaxed[x + 1]
        total = relaxed[x] + relaxed[x + 2] + around(center, 0) + around(center, 1)
        value = total + rho[x + 1] * inverse - ion_charge(center) + screening * center
        potential_ref[x] = value[PAD:PAD + half] * (1.0 / (6.0 + screening))

    loop(1, layers - 1, second)
    for copy in rho_copies:
        copy.wait_recv()
    relax_once(0)
    relax_once(layers + 1)
    both(second)

    for copy in sent:
        copy.wait_send()
    pltpu.make_async_copy(others, others, sum_send).wait()


def ion_charge(value):
    return (2.0 * screening) * jnp.tanh(0.5 * value)


def body(ends, slabs, w_field, psi_init, start_field, charges):
    layers, rows, depth = w_field.shape
    half = rows // ends
    wide = half + 2 * PAD
    devices = ends * slabs
    out = jax.ShapeDtypeStruct((layers, half, depth), jnp.float32)
    dma = pltpu.SemaphoreType.DMA

    def tile(*lead):
        return pltpu.VMEM((*lead, wide, depth), jnp.float32)

    hbm = pl.BlockSpec(memory_space=pl.ANY)
    vmem = pl.BlockSpec(memory_space=pltpu.VMEM)
    return pl.pallas_call(
        functools.partial(kernel, ends, slabs),
        out_shape=(out, out),
        in_specs=[pl.BlockSpec(memory_space=pltpu.SMEM), hbm, hbm, hbm],
        out_specs=(vmem, vmem),
        scratch_shapes=[
            tile(layers), tile(layers + 4), tile(2, layers), tile(NS, layers),
            tile(2, NS, layers + 2), tile(2, NS + 1, layers), tile(layers), tile(layers + 2),
            tile(layers + 2), tile(layers + 2), pltpu.VMEM((devices, 1, 128), jnp.float32),
            dma((3, 3)), dma((layers, 3)), dma((layers, 3)), dma((2, 3)), dma((2, 3)),
            dma((2, NS, 2)), dma((2, NS, 2)), dma((2,)), dma((2,)), dma(()), dma(()),
        ],
        compiler_params=pltpu.CompilerParams(
            collective_id=0, has_side_effects=True, vmem_limit_bytes=56 * 1024 * 1024
        ),
        name="scf_step",
    )(charges, w_field, psi_init, start_field)


def solution(mesh):
    in_specs = (P("slab", None, None), P("slab", None, None), P("end", "slab", None, None), P())
    out_specs = (P("slab", "end", None), P("slab", "end", None))
    step = functools.partial(body, mesh.shape["end"], mesh.shape["slab"])
    return jax.shard_map(step, mesh=mesh, in_specs=in_specs, out_specs=out_specs, check_vma=False)
```

```python
import functools

import jax
import jax.numpy as jnp
from jax import lax
from jax.experimental import pallas as pl
from jax.experimental.pallas import tpu as pltpu
from jax.sharding import PartitionSpec as P

NS = 4
PAD = 8
mobility = 0.15
screening = 1.0
OWN, FOREIGN = 0, 1
MESH = pl.DeviceIdType.MESH


def kernel(ends, slabs, charges_ref, w_hbm, psi_hbm, start_hbm, density_ref, potential_ref,
           w_v, psi_v, start_v, factor, u, rounded, phi, rho, base, relaxed, sums,
           gate, local_sem, field_send, field_recv, psi_send, psi_recv, halo_send, halo_recv,
           rho_send, rho_recv, sum_send, sum_recv):
    side, slab = lax.axis_index("end"), lax.axis_index("slab")
    other = lax.rem(side + 1, ends)
    left = (side, lax.rem(slab + slabs - 1, slabs))
    right = (side, lax.rem(slab + 1, slabs))
    partner = (other, slab)
    layers, rows = w_hbm.shape[0], w_hbm.shape[1]
    half = rows // ends
    devices = ends * slabs
    flat = side * slabs + slab
    delta = 1.0 / NS

    def device(step):
        target = lax.rem(flat + step, devices)
        return (target // slabs, lax.rem(target, slabs))

    barrier = pltpu.get_barrier_semaphore()

    near = []
    width = 1
    while width < slabs:
        near.append((side, slab + width - 2 * width * lax.rem(slab // width, 2)))
        width *= 2
    near.append(partner)
    for neighbour in near:
        pl.semaphore_signal(barrier, inc=1, device_id=neighbour, device_id_type=MESH)

    def pieces(which):
        first = which * half
        return (
            (pl.multiple_of(first, 8), PAD, half),
            (pl.multiple_of(lax.rem(first + rows - PAD, rows), 8), 0, PAD),
            (pl.multiple_of(lax.rem(first + half, rows), 8), PAD + half, PAD),
        )

    mine, theirs = pieces(side), pieces(other)
    local = []
    for k, (source, target, first) in enumerate(
        ((w_hbm, w_v, 0), (psi_hbm, psi_v, 2), (start_hbm.at[0], start_v.at[OWN], 0))
    ):
        for n, (begin, at, count) in enumerate(mine):
            local.append(
                pltpu.make_async_copy(
                    source.at[:, pl.ds(begin, count)],
                    target.at[pl.ds(first, layers), pl.ds(at, count)],
                    local_sem.at[k, n],
                )
            )
    for copy in local:
        copy.start()

    q = [charges_ref[side * (NS - 2 * t) + t].astype(jnp.float32) for t in range(NS + 1)]
    pair = [0.5 * (q[k] + q[k + 1]) for k in range(NS)]

    def make_factor(x, carry):
        w, psi = w_v[x], psi_v[x + 2]
        for k in range(NS):
            factor[k, x] = jnp.exp(-0.5 * delta * (w + pair[k] * psi))
        return carry

    def index(chain, t):
        return t if chain == OWN else NS - 1 - t

    def begin_chain(chain, x):
        value = start_v[chain, x]
        rounded[chain, 0, x] = value.astype(jnp.bfloat16).astype(jnp.float32)
        u[chain, 0, x + 1] = factor[index(chain, 0), x] * value

    def around(value, axis):
        return pltpu.roll(value, 1, axis) + pltpu.roll(value, value.shape[axis] - 1, axis)

    def advanced(chain, t, x):
        center = u[chain, t, x + 1]
        total = u[chain, t, x] + u[chain, t, x + 2] + around(center, 0) + around(center, 1)
        return factor[index(chain, t), x] * (center + mobility * (total - 6.0 * center))

    def advance(chain, t, x):
        value = advanced(chain, t, x)
        rounded[chain, t + 1, x] = value.astype(jnp.bfloat16).astype(jnp.float32)
        if t + 1 < NS:
            u[chain, t + 1, x + 1] = factor[index(chain, t + 1), x] * value

    def loop(low, high, step):
        def body(x, carry):
            step(x)
            return carry

        lax.fori_loop(low, high, body, 0)

    def both(step):
        step(0)
        step(layers - 1)

    def halo(chain, t):
        return (
            pltpu.make_async_remote_copy(
                u.at[chain, t, 1], u.at[chain, t, layers + 1],
                halo_send.at[chain, t, 0], halo_recv.at[chain, t, 0],
                device_id=left, device_id_type=MESH,
            ),
            pltpu.make_async_remote_copy(
                u.at[chain, t, layers], u.at[chain, t, 0],
                halo_send.at[chain, t, 1], halo_recv.at[chain, t, 1],
                device_id=right, device_id_type=MESH,
            ),
        )

    sent = []

    def send_halo(chain, t):
        for copy in halo(chain, t):
            copy.start()
            sent.append(copy)

    def wait_halo(chain, t):
        for copy in halo(chain, t):
            copy.wait_recv()

    groups = [(0, layers - 1), (1, layers - 2), (2, layers - 3), tuple(range(3, layers - 3))]
    order = [x for group in groups for x in group]

    def field(x):
        return [
            pltpu.make_async_remote_copy(
                start_hbm.at[0, x, pl.ds(begin, count)],
                start_v.at[FOREIGN, x, pl.ds(at, count)],
                field_send.at[x, n], field_recv.at[x, n],
                device_id=partner, device_id_type=MESH,
            )
            for n, (begin, at, count) in enumerate(theirs)
        ]

    def arrive(group):
        for x in groups[group]:
            for copy in field(x):
                copy.wait_recv()
        for x in groups[group]:
            begin_chain(FOREIGN, x)

    def psi_halo():
        copies = []
        for n, (begin, at, count) in enumerate(mine):
            copies.append(
                pltpu.make_async_remote_copy(
                    psi_hbm.at[pl.ds(0, 2), pl.ds(begin, count)],
                    psi_v.at[pl.ds(layers + 2, 2), pl.ds(at, count)],
                    psi_send.at[0, n], psi_recv.at[0, n],
                    device_id=left, device_id_type=MESH,
                )
            )
            copies.append(
                pltpu.make_async_remote_copy(
                    psi_hbm.at[pl.ds(layers - 2, 2), pl.ds(begin, count)],
                    psi_v.at[pl.ds(0, 2), pl.ds(at, count)],
                    psi_send.at[1, n], psi_recv.at[1, n],
                    device_id=right, device_id_type=MESH,
                )
            )
        return copies

    pl.semaphore_wait(barrier, len(near))
    for x in order:
        for copy in field(x):
            copy.start()
            sent.append(copy)
    for copy in local:
        copy.wait()
    stages = len(near)
    for stage, neighbour in enumerate(near):
        pl.semaphore_signal(gate.at[stage], inc=1, device_id=neighbour, device_id_type=MESH)
        low, high = layers * stage // stages, layers * (stage + 1) // stages
        lax.fori_loop(low, high, make_factor, 0)
        loop(low, high, functools.partial(begin_chain, OWN))
        pl.semaphore_wait(gate.at[stage], 1)
    send_halo(OWN, 0)
    psi_copies = psi_halo()
    for copy in psi_copies:
        copy.start()
        sent.append(copy)
    loop(1, layers - 1, functools.partial(advance, OWN, 0))

    arrive(0)
    send_halo(FOREIGN, 0)
    wait_halo(OWN, 0)
    both(functools.partial(advance, OWN, 0))
    send_halo(OWN, 1)
    loop(1, layers - 1, functools.partial(advance, OWN, 1))

    arrive(1)
    wait_halo(FOREIGN, 0)
    both(functools.partial(advance, FOREIGN, 0))
    send_halo(FOREIGN, 1)
    wait_halo(OWN, 1)
    both(functools.partial(advance, OWN, 1))
    send_halo(OWN, 2)
    loop(1, layers - 1, functools.partial(advance, OWN, 2))

    arrive(2)
    for x in (1, layers - 2):
        advance(FOREIGN, 0, x)
    wait_halo(FOREIGN, 1)
    both(functools.partial(advance, FOREIGN, 1))
    send_halo(FOREIGN, 2)
    wait_halo(OWN, 2)
    both(functools.partial(advance, OWN, 2))
    send_halo(OWN, 3)
    loop(1, layers - 1, functools.partial(advance, OWN, 3))

    arrive(3)
    for x in (2, layers - 3):
        advance(FOREIGN, 0, x)
    for x in (1, layers - 2):
        advance(FOREIGN, 1, x)
    wait_halo(FOREIGN, 2)
    both(functools.partial(advance, FOREIGN, 2))
    send_halo(FOREIGN, 3)
    loop(3, layers - 3, functools.partial(advance, FOREIGN, 0))
    loop(2, layers - 2, functools.partial(advance, FOREIGN, 1))
    loop(1, layers - 1, functools.partial(advance, FOREIGN, 2))
    wait_halo(OWN, 3)
    both(functools.partial(advance, OWN, 3))

    weights = [delta * (0.5 if t in (0, NS) else 1.0) for t in range(NS + 1)]
    charged = [weights[t] * q[t] for t in range(NS + 1)]

    def gather(x):
        phi_layer, rho_layer = 0.0, 0.0
        for t in range(1, NS + 1):
            product = rounded[OWN, t, x] * rounded[FOREIGN, NS - t, x]
            phi_layer = phi_layer + weights[t] * product
            rho_layer = rho_layer + charged[t] * product
        phi[x] = phi_layer
        rho[x + 1] = rho_layer

    def finish(x):
        value = advanced(FOREIGN, NS - 1, x).astype(jnp.bfloat16).astype(jnp.float32)
        product = rounded[OWN, 0, x] * value
        phi[x] += weights[0] * product
        rho[x + 1] += charged[0] * product

    loop(0, layers, gather)
    loop(1, layers - 1, finish)

    for copy in psi_copies:
        copy.wait_recv()

    def make_base(x):
        center = psi_v[x + 1]
        total = psi_v[x] + psi_v[x + 2] + around(center, 0) + around(center, 1)
        base[x] = total - ion_charge(center) + screening * center

    loop(0, layers + 2, make_base)

    inner = pl.ds(PAD, half)

    def add(x, carry):
        return carry + phi[x, inner]

    partial = lax.fori_loop(2, layers - 1, add, phi[1, inner])
    wait_halo(FOREIGN, NS - 1)
    both(finish)
    rho_copies = (
        pltpu.make_async_remote_copy(
            rho.at[1, inner], rho.at[layers + 1, inner], rho_send.at[0], rho_recv.at[0],
            device_id=left, device_id_type=MESH,
        ),
        pltpu.make_async_remote_copy(
            rho.at[layers, inner], rho.at[0, inner], rho_send.at[1], rho_recv.at[1],
            device_id=right, device_id_type=MESH,
        ),
    )
    partial = partial + phi[0, inner] + phi[layers - 1, inner]
    sums[0] = jnp.sum(
        sum(partial[:, k:k + 128] for k in range(0, partial.shape[1], 128)), axis=0, keepdims=True
    )

    def share(step, carry):
        pltpu.make_async_remote_copy(
            sums.at[0], sums.at[step], sum_send, sum_recv,
            device_id=device(step), device_id_type=MESH,
        ).start()
        return carry

    lax.fori_loop(1, devices, share, 0)
    for copy in rho_copies:
        copy.start()
        sent.append(copy)

    others = sums.at[pl.ds(1, devices - 1)]
    pltpu.make_async_copy(others, others, sum_recv).wait()
    cells = float(devices * layers * half * w_hbm.shape[2])
    inverse = cells / jnp.sum(sums[...])

    def relax_once(x):
        relaxed[x] = (base[x] + rho[x] * inverse) * (1.0 / (6.0 + screening))

    def first(x):
        density_ref[x] = phi[x, inner] * inverse
        relax_once(x + 1)

    loop(0, layers, first)

    def second(x):
        center = relaxed[x + 1]
        total = relaxed[x] + relaxed[x + 2] + around(center, 0) + around(center, 1)
        value = total + rho[x + 1] * inverse - ion_charge(center) + screening * center
        potential_ref[x] = value[PAD:PAD + half] * (1.0 / (6.0 + screening))

    loop(1, layers - 1, second)
    for copy in rho_copies:
        copy.wait_recv()
    relax_once(0)
    relax_once(layers + 1)
    both(second)

    for copy in sent:
        copy.wait_send()
    pltpu.make_async_copy(others, others, sum_send).wait()


def ion_charge(value):
    return (2.0 * screening) * jnp.tanh(0.5 * value)


def body(ends, slabs, w_field, psi_init, start_field, charges):
    layers, rows, depth = w_field.shape
    half = rows // ends
    wide = half + 2 * PAD
    devices = ends * slabs
    stages = slabs.bit_length()
    out = jax.ShapeDtypeStruct((layers, half, depth), jnp.float32)
    dma = pltpu.SemaphoreType.DMA

    def tile(*lead):
        return pltpu.VMEM((*lead, wide, depth), jnp.float32)

    hbm = pl.BlockSpec(memory_space=pltpu.HBM)
    vmem = pl.BlockSpec(memory_space=pltpu.VMEM)
    return pl.pallas_call(
        functools.partial(kernel, ends, slabs),
        out_shape=(out, out),
        in_specs=[pl.BlockSpec(memory_space=pltpu.SMEM), hbm, hbm, hbm],
        out_specs=(vmem, vmem),
        scratch_shapes=[
            tile(layers), tile(layers + 4), tile(2, layers), tile(NS, layers),
            tile(2, NS, layers + 2), tile(2, NS + 1, layers), tile(layers), tile(layers + 2),
            tile(layers + 2), tile(layers + 2), pltpu.VMEM((devices, 1, 128), jnp.float32),
            pltpu.SemaphoreType.REGULAR((stages,)), dma((3, 3)), dma((layers, 3)), dma((layers, 3)), dma((2, 3)), dma((2, 3)),
            dma((2, NS, 2)), dma((2, NS, 2)), dma((2,)), dma((2,)), dma(()), dma(()),
        ],
        compiler_params=pltpu.CompilerParams(
            collective_id=0, has_side_effects=True, vmem_limit_bytes=30 * 1024 * 1024
        ),
        name="scf_step",
    )(charges, w_field, psi_init, start_field)


def solution(mesh):
    in_specs = (P("slab", None, None), P("slab", None, None), P("end", "slab", None, None), P())
    out_specs = (P("slab", "end", None), P("slab", "end", None))
    step = functools.partial(body, mesh.shape["end"], mesh.shape["slab"])
    return jax.shard_map(step, mesh=mesh, in_specs=in_specs, out_specs=out_specs, check_vma=False)
```

```python
import functools

import jax
import jax.numpy as jnp
from jax import lax
from jax.experimental import pallas as pl
from jax.experimental.pallas import tpu as pltpu
from jax.sharding import PartitionSpec as P

NS = 4
PAD = 8
mobility = 0.15
screening = 1.0
OWN, FOREIGN = 0, 1
MESH = pl.DeviceIdType.MESH


def kernel(ends, slabs, charges_ref, w_hbm, psi_hbm, start_hbm, density_ref, potential_ref,
           w_v, psi_v, start_v, factor, u, rounded, phi, rho, base, relaxed, sums,
           gate, local_sem, field_send, field_recv, psi_send, psi_recv, halo_send, halo_recv,
           rho_send, rho_recv, sum_send, sum_recv):
    side, slab = lax.axis_index("end"), lax.axis_index("slab")
    other = lax.rem(side + 1, ends)
    left = (side, lax.rem(slab + slabs - 1, slabs))
    right = (side, lax.rem(slab + 1, slabs))
    partner = (other, slab)
    layers, rows = w_hbm.shape[0], w_hbm.shape[1]
    half = rows // ends
    devices = ends * slabs
    flat = side * slabs + slab
    delta = 1.0 / NS

    def device(step):
        target = lax.rem(flat + step, devices)
        return (target // slabs, lax.rem(target, slabs))

    barrier = pltpu.get_barrier_semaphore()

    near = []
    width = 1
    while width < slabs:
        near.append((side, slab + width - 2 * width * lax.rem(slab // width, 2)))
        width *= 2
    near.append(partner)
    for neighbour in near:
        pl.semaphore_signal(barrier, inc=1, device_id=neighbour, device_id_type=MESH)

    def pieces(which):
        first = which * half
        return (
            (pl.multiple_of(first, 8), PAD, half),
            (pl.multiple_of(lax.rem(first + rows - PAD, rows), 8), 0, PAD),
            (pl.multiple_of(lax.rem(first + half, rows), 8), PAD + half, PAD),
        )

    mine, theirs = pieces(side), pieces(other)
    local = []
    for k, (source, target, first) in enumerate(
        ((w_hbm, w_v, 0), (psi_hbm, psi_v, 2), (start_hbm.at[0], start_v.at[OWN], 0))
    ):
        for n, (begin, at, count) in enumerate(mine):
            local.append(
                pltpu.make_async_copy(
                    source.at[:, pl.ds(begin, count)],
                    target.at[pl.ds(first, layers), pl.ds(at, count)],
                    local_sem.at[k, n],
                )
            )
    for copy in local:
        copy.start()

    q = [charges_ref[side * (NS - 2 * t) + t].astype(jnp.float32) for t in range(NS + 1)]
    pair = [0.5 * (q[k] + q[k + 1]) for k in range(NS)]

    def make_factor(x, carry):
        w, psi = w_v[x], psi_v[x + 2]
        for k in range(NS):
            factor[k, x] = jnp.exp(-0.5 * delta * (w + pair[k] * psi))
        return carry

    def index(chain, t):
        return t if chain == OWN else NS - 1 - t

    def begin_chain(chain, x):
        value = start_v[chain, x]
        rounded[chain, 0, x] = value.astype(jnp.bfloat16).astype(jnp.float32)
        u[chain, 0, x + 1] = factor[index(chain, 0), x] * value

    def around(value, axis):
        return pltpu.roll(value, 1, axis) + pltpu.roll(value, value.shape[axis] - 1, axis)

    def advanced(chain, t, x):
        center = u[chain, t, x + 1]
        total = u[chain, t, x] + u[chain, t, x + 2] + around(center, 0) + around(center, 1)
        return factor[index(chain, t), x] * (center + mobility * (total - 6.0 * center))

    def advance(chain, t, x):
        value = advanced(chain, t, x)
        rounded[chain, t + 1, x] = value.astype(jnp.bfloat16).astype(jnp.float32)
        if t + 1 < NS:
            u[chain, t + 1, x + 1] = factor[index(chain, t + 1), x] * value

    def loop(low, high, step):
        def body(x, carry):
            step(x)
            return carry

        lax.fori_loop(low, high, body, 0)

    def both(step):
        step(0)
        step(layers - 1)

    def halo(chain, t):
        return (
            pltpu.make_async_remote_copy(
                u.at[chain, t, 1], u.at[chain, t, layers + 1],
                halo_send.at[chain, t, 0], halo_recv.at[chain, t, 0],
                device_id=left, device_id_type=MESH,
            ),
            pltpu.make_async_remote_copy(
                u.at[chain, t, layers], u.at[chain, t, 0],
                halo_send.at[chain, t, 1], halo_recv.at[chain, t, 1],
                device_id=right, device_id_type=MESH,
            ),
        )

    sent = []

    def send_halo(chain, t):
        for copy in halo(chain, t):
            copy.start()
            sent.append(copy)

    def wait_halo(chain, t):
        for copy in halo(chain, t):
            copy.wait_recv()

    groups = [(0, layers - 1), (1, layers - 2), (2, layers - 3), tuple(range(3, layers - 3))]
    order = [x for group in groups for x in group]

    def field(x):
        return [
            pltpu.make_async_remote_copy(
                start_hbm.at[0, x, pl.ds(begin, count)],
                start_v.at[FOREIGN, x, pl.ds(at, count)],
                field_send.at[x, n], field_recv.at[x, n],
                device_id=partner, device_id_type=MESH,
            )
            for n, (begin, at, count) in enumerate(theirs)
        ]

    def arrive(group):
        for x in groups[group]:
            for copy in field(x):
                copy.wait_recv()
        for x in groups[group]:
            begin_chain(FOREIGN, x)

    def psi_halo():
        copies = []
        for n, (begin, at, count) in enumerate(mine):
            deep = 2 if count == half else 1
            copies.append(
                pltpu.make_async_remote_copy(
                    psi_hbm.at[pl.ds(0, deep), pl.ds(begin, count)],
                    psi_v.at[pl.ds(layers + 2, deep), pl.ds(at, count)],
                    psi_send.at[0, n], psi_recv.at[0, n],
                    device_id=left, device_id_type=MESH,
                )
            )
            copies.append(
                pltpu.make_async_remote_copy(
                    psi_hbm.at[pl.ds(layers - deep, deep), pl.ds(begin, count)],
                    psi_v.at[pl.ds(2 - deep, deep), pl.ds(at, count)],
                    psi_send.at[1, n], psi_recv.at[1, n],
                    device_id=right, device_id_type=MESH,
                )
            )
        return copies

    pl.semaphore_wait(barrier, len(near))
    for x in order:
        for copy in field(x):
            copy.start()
            sent.append(copy)
    for copy in local:
        copy.wait()
    stages = len(near)
    for stage, neighbour in enumerate(near):
        pl.semaphore_signal(gate.at[stage], inc=1, device_id=neighbour, device_id_type=MESH)
        low, high = layers * stage // stages, layers * (stage + 1) // stages
        lax.fori_loop(low, high, make_factor, 0)
        loop(low, high, functools.partial(begin_chain, OWN))
        if neighbour is not partner:
            pl.semaphore_wait(gate.at[stage], 1)
    send_halo(OWN, 0)
    loop(1, layers - 1, functools.partial(advance, OWN, 0))

    arrive(0)
    send_halo(FOREIGN, 0)
    wait_halo(OWN, 0)
    both(functools.partial(advance, OWN, 0))
    send_halo(OWN, 1)
    loop(1, layers - 1, functools.partial(advance, OWN, 1))

    arrive(1)
    wait_halo(FOREIGN, 0)
    both(functools.partial(advance, FOREIGN, 0))
    send_halo(FOREIGN, 1)
    wait_halo(OWN, 1)
    both(functools.partial(advance, OWN, 1))
    send_halo(OWN, 2)
    loop(1, layers - 1, functools.partial(advance, OWN, 2))

    arrive(2)
    for x in (1, layers - 2):
        advance(FOREIGN, 0, x)
    wait_halo(FOREIGN, 1)
    both(functools.partial(advance, FOREIGN, 1))
    send_halo(FOREIGN, 2)
    wait_halo(OWN, 2)
    both(functools.partial(advance, OWN, 2))
    send_halo(OWN, 3)
    loop(1, layers - 1, functools.partial(advance, OWN, 3))

    arrive(3)
    for x in (2, layers - 3):
        advance(FOREIGN, 0, x)
    for x in (1, layers - 2):
        advance(FOREIGN, 1, x)
    wait_halo(FOREIGN, 2)
    both(functools.partial(advance, FOREIGN, 2))
    send_halo(FOREIGN, 3)
    psi_copies = psi_halo()
    for copy in psi_copies:
        copy.start()
        sent.append(copy)
    loop(3, layers - 3, functools.partial(advance, FOREIGN, 0))
    loop(2, layers - 2, functools.partial(advance, FOREIGN, 1))
    loop(1, layers - 1, functools.partial(advance, FOREIGN, 2))
    wait_halo(OWN, 3)
    both(functools.partial(advance, OWN, 3))

    weights = [delta * (0.5 if t in (0, NS) else 1.0) for t in range(NS + 1)]
    charged = [weights[t] * q[t] for t in range(NS + 1)]

    def gather(x):
        phi_layer, rho_layer = 0.0, 0.0
        for t in range(1, NS + 1):
            product = rounded[OWN, t, x] * rounded[FOREIGN, NS - t, x]
            phi_layer = phi_layer + weights[t] * product
            rho_layer = rho_layer + charged[t] * product
        phi[x] = phi_layer
        rho[x + 1] = rho_layer

    def finish(x):
        value = advanced(FOREIGN, NS - 1, x).astype(jnp.bfloat16).astype(jnp.float32)
        product = rounded[OWN, 0, x] * value
        phi[x] += weights[0] * product
        rho[x + 1] += charged[0] * product

    loop(0, layers, gather)
    loop(1, layers - 1, finish)

    inner = pl.ds(PAD, half)

    def add(x, carry):
        return carry + phi[x, inner]

    partial = lax.fori_loop(2, layers - 1, add, phi[1, inner])
    wait_halo(FOREIGN, NS - 1)
    both(finish)
    rho_copies = (
        pltpu.make_async_remote_copy(
            rho.at[1, inner], rho.at[layers + 1, inner], rho_send.at[0], rho_recv.at[0],
            device_id=left, device_id_type=MESH,
        ),
        pltpu.make_async_remote_copy(
            rho.at[layers, inner], rho.at[0, inner], rho_send.at[1], rho_recv.at[1],
            device_id=right, device_id_type=MESH,
        ),
    )
    partial = partial + phi[0, inner] + phi[layers - 1, inner]
    sums[0] = jnp.sum(
        sum(partial[:, k:k + 128] for k in range(0, partial.shape[1], 128)), axis=0, keepdims=True
    )

    def share(step, carry):
        pltpu.make_async_remote_copy(
            sums.at[0], sums.at[step], sum_send, sum_recv,
            device_id=device(step), device_id_type=MESH,
        ).start()
        return carry

    pl.semaphore_wait(gate.at[stages - 1], 1)
    lax.fori_loop(1, devices, share, 0)
    for copy in rho_copies:
        copy.start()
        sent.append(copy)

    for copy in psi_copies:
        copy.wait_recv()

    def make_base(x):
        center = psi_v[x + 1]
        total = psi_v[x] + psi_v[x + 2] + around(center, 0) + around(center, 1)
        base[x] = total - ion_charge(center) + screening * center

    loop(0, layers + 2, make_base)

    others = sums.at[pl.ds(1, devices - 1)]
    pltpu.make_async_copy(others, others, sum_recv).wait()
    cells = float(devices * layers * half * w_hbm.shape[2])
    inverse = cells / jnp.sum(sums[...])

    def relax_once(x):
        relaxed[x] = (base[x] + rho[x] * inverse) * (1.0 / (6.0 + screening))

    def first(x):
        density_ref[x] = phi[x, inner] * inverse
        relax_once(x + 1)

    loop(0, layers, first)

    def second(x):
        center = relaxed[x + 1]
        total = relaxed[x] + relaxed[x + 2] + around(center, 0) + around(center, 1)
        value = total + rho[x + 1] * inverse - ion_charge(center) + screening * center
        potential_ref[x] = value[PAD:PAD + half] * (1.0 / (6.0 + screening))

    loop(1, layers - 1, second)
    for copy in rho_copies:
        copy.wait_recv()
    relax_once(0)
    relax_once(layers + 1)
    both(second)

    for copy in sent:
        copy.wait_send()
    pltpu.make_async_copy(others, others, sum_send).wait()


def ion_charge(value):
    return (2.0 * screening) * jnp.tanh(0.5 * value)


def body(ends, slabs, w_field, psi_init, start_field, charges):
    layers, rows, depth = w_field.shape
    half = rows // ends
    wide = half + 2 * PAD
    devices = ends * slabs
    stages = slabs.bit_length()
    out = jax.ShapeDtypeStruct((layers, half, depth), jnp.float32)
    dma = pltpu.SemaphoreType.DMA

    def tile(*lead):
        return pltpu.VMEM((*lead, wide, depth), jnp.float32)

    hbm = pl.BlockSpec(memory_space=pltpu.HBM)
    vmem = pl.BlockSpec(memory_space=pltpu.VMEM)
    return pl.pallas_call(
        functools.partial(kernel, ends, slabs),
        out_shape=(out, out),
        in_specs=[pl.BlockSpec(memory_space=pltpu.SMEM), hbm, hbm, hbm],
        out_specs=(vmem, vmem),
        scratch_shapes=[
            tile(layers), tile(layers + 4), tile(2, layers), tile(NS, layers),
            tile(2, NS, layers + 2), tile(2, NS + 1, layers), tile(layers), tile(layers + 2),
            tile(layers + 2), tile(layers + 2), pltpu.VMEM((devices, 1, 128), jnp.float32),
            pltpu.SemaphoreType.REGULAR((stages,)), dma((3, 3)), dma((layers, 3)), dma((layers, 3)), dma((2, 3)), dma((2, 3)),
            dma((2, NS, 2)), dma((2, NS, 2)), dma((2,)), dma((2,)), dma(()), dma(()),
        ],
        compiler_params=pltpu.CompilerParams(
            collective_id=0, has_side_effects=True, vmem_limit_bytes=30 * 1024 * 1024
        ),
        name="scf_step",
    )(charges, *[pltpu.with_memory_space_constraint(v, pltpu.HBM) for v in (w_field, psi_init, start_field)])


def solution(mesh):
    in_specs = (P("slab", None, None), P("slab", None, None), P("end", "slab", None, None), P())
    out_specs = (P("slab", "end", None), P("slab", "end", None))
    step = functools.partial(body, mesh.shape["end"], mesh.shape["slab"])
    return jax.shard_map(step, mesh=mesh, in_specs=in_specs, out_specs=out_specs, check_vma=False)
```

```python
import functools

import jax
import jax.numpy as jnp
from jax import lax
from jax.experimental import pallas as pl
from jax.experimental.pallas import tpu as pltpu
from jax.sharding import PartitionSpec as P

NS = 4
PAD = 8
mobility = 0.15
screening = 1.0
OWN, FOREIGN = 0, 1
MESH = pl.DeviceIdType.MESH


def kernel(ends, slabs, charges_ref, w_hbm, psi_hbm, start_hbm, density_ref, potential_ref,
           w_v, psi_v, start_v, factor, u, rounded, phi, rho, base, relaxed, sums,
           gate, local_sem, field_send, field_recv, psi_send, psi_recv, halo_send, halo_recv,
           rho_send, rho_recv, sum_send, sum_recv):
    side, slab = lax.axis_index("end"), lax.axis_index("slab")
    other = lax.rem(side + 1, ends)
    left = (side, lax.rem(slab + slabs - 1, slabs))
    right = (side, lax.rem(slab + 1, slabs))
    partner = (other, slab)
    layers, rows = w_hbm.shape[0], w_hbm.shape[1]
    half = rows // ends
    devices = ends * slabs
    flat = side * slabs + slab
    delta = 1.0 / NS

    def device(step):
        target = lax.rem(flat + step, devices)
        return (target // slabs, lax.rem(target, slabs))

    barrier = pltpu.get_barrier_semaphore()

    near = []
    width = 1
    while width < slabs:
        near.append((side, slab + width - 2 * width * lax.rem(slab // width, 2)))
        width *= 2
    near.append(partner)
    for neighbour in near:
        pl.semaphore_signal(barrier, inc=1, device_id=neighbour, device_id_type=MESH)

    def pieces(which):
        first = which * half
        return (
            (pl.multiple_of(first, 8), PAD, half),
            (pl.multiple_of(lax.rem(first + rows - PAD, rows), 8), 0, PAD),
            (pl.multiple_of(lax.rem(first + half, rows), 8), PAD + half, PAD),
        )

    mine, theirs = pieces(side), pieces(other)
    local = []
    for k, (source, target, first) in enumerate(
        ((w_hbm, w_v, 0), (psi_hbm, psi_v, 2), (start_hbm.at[0], start_v.at[OWN], 0))
    ):
        for n, (begin, at, count) in enumerate(mine):
            local.append(
                pltpu.make_async_copy(
                    source.at[:, pl.ds(begin, count)],
                    target.at[pl.ds(first, layers), pl.ds(at, count)],
                    local_sem.at[k, n],
                )
            )
    for copy in local:
        copy.start()

    q = [charges_ref[side * (NS - 2 * t) + t].astype(jnp.float32) for t in range(NS + 1)]
    pair = [0.5 * (q[k] + q[k + 1]) for k in range(NS)]

    def make_factor(x, carry):
        w, psi = w_v[x], psi_v[x + 2]
        for k in range(NS):
            factor[k, x] = jnp.exp(-0.5 * delta * (w + pair[k] * psi))
        return carry

    def index(chain, t):
        return t if chain == OWN else NS - 1 - t

    def begin_chain(chain, x):
        value = start_v[chain, x]
        rounded[chain, 0, x] = value.astype(jnp.bfloat16).astype(jnp.float32)
        u[chain, 0, x + 1] = factor[index(chain, 0), x] * value

    def around(value, axis):
        return pltpu.roll(value, 1, axis) + pltpu.roll(value, value.shape[axis] - 1, axis)

    def advanced(chain, t, x):
        center = u[chain, t, x + 1]
        total = u[chain, t, x] + u[chain, t, x + 2] + around(center, 0) + around(center, 1)
        return factor[index(chain, t), x] * (center + mobility * (total - 6.0 * center))

    def advance(chain, t, x):
        value = advanced(chain, t, x)
        rounded[chain, t + 1, x] = value.astype(jnp.bfloat16).astype(jnp.float32)
        if t + 1 < NS:
            u[chain, t + 1, x + 1] = factor[index(chain, t + 1), x] * value

    def loop(low, high, step):
        def body(x, carry):
            step(x)
            return carry

        lax.fori_loop(low, high, body, 0)

    def both(step):
        step(0)
        step(layers - 1)

    def halo(chain, t):
        return (
            pltpu.make_async_remote_copy(
                u.at[chain, t, 1], u.at[chain, t, layers + 1],
                halo_send.at[chain, t, 0], halo_recv.at[chain, t, 0],
                device_id=left, device_id_type=MESH,
            ),
            pltpu.make_async_remote_copy(
                u.at[chain, t, layers], u.at[chain, t, 0],
                halo_send.at[chain, t, 1], halo_recv.at[chain, t, 1],
                device_id=right, device_id_type=MESH,
            ),
        )

    sent = []

    def send_halo(chain, t):
        for copy in halo(chain, t):
            copy.start()
            sent.append(copy)

    def wait_halo(chain, t):
        for copy in halo(chain, t):
            copy.wait_recv()

    groups = [(0, layers - 1), (1, layers - 2), (2, layers - 3), tuple(range(3, layers - 3))]
    order = [x for group in groups for x in group]

    def field(x):
        return [
            pltpu.make_async_remote_copy(
                start_hbm.at[0, x, pl.ds(begin, count)],
                start_v.at[FOREIGN, x, pl.ds(at, count)],
                field_send.at[x, n], field_recv.at[x, n],
                device_id=partner, device_id_type=MESH,
            )
            for n, (begin, at, count) in enumerate(theirs)
        ]

    def arrive(group):
        for x in groups[group]:
            for copy in field(x):
                copy.wait_recv()
        for x in groups[group]:
            begin_chain(FOREIGN, x)

    def psi_halo():
        copies = []
        for n, (begin, at, count) in enumerate(mine):
            deep = 2 if count == half else 1
            copies.append(
                pltpu.make_async_remote_copy(
                    psi_hbm.at[pl.ds(0, deep), pl.ds(begin, count)],
                    psi_v.at[pl.ds(layers + 2, deep), pl.ds(at, count)],
                    psi_send.at[0, n], psi_recv.at[0, n],
                    device_id=left, device_id_type=MESH,
                )
            )
            copies.append(
                pltpu.make_async_remote_copy(
                    psi_hbm.at[pl.ds(layers - deep, deep), pl.ds(begin, count)],
                    psi_v.at[pl.ds(2 - deep, deep), pl.ds(at, count)],
                    psi_send.at[1, n], psi_recv.at[1, n],
                    device_id=right, device_id_type=MESH,
                )
            )
        return copies

    pl.semaphore_wait(barrier, len(near))
    for x in order:
        for copy in field(x):
            copy.start()
            sent.append(copy)
    for copy in local:
        copy.wait()
    stages = len(near)
    for stage, neighbour in enumerate(near):
        pl.semaphore_signal(gate.at[stage], inc=1, device_id=neighbour, device_id_type=MESH)
        low, high = layers * stage // stages, layers * (stage + 1) // stages
        lax.fori_loop(low, high, make_factor, 0)
        loop(low, high, functools.partial(begin_chain, OWN))
        if neighbour is not partner:
            pl.semaphore_wait(gate.at[stage], 1)
    send_halo(OWN, 0)
    loop(1, layers - 1, functools.partial(advance, OWN, 0))

    def make_base(x):
        center = psi_v[x + 1]
        total = psi_v[x] + psi_v[x + 2] + around(center, 0) + around(center, 1)
        base[x] = total - ion_charge(center) + screening * center

    loop(2, layers, make_base)

    arrive(0)
    send_halo(FOREIGN, 0)
    wait_halo(OWN, 0)
    both(functools.partial(advance, OWN, 0))
    send_halo(OWN, 1)
    loop(1, layers - 1, functools.partial(advance, OWN, 1))

    arrive(1)
    wait_halo(FOREIGN, 0)
    both(functools.partial(advance, FOREIGN, 0))
    send_halo(FOREIGN, 1)
    wait_halo(OWN, 1)
    both(functools.partial(advance, OWN, 1))
    send_halo(OWN, 2)
    loop(1, layers - 1, functools.partial(advance, OWN, 2))

    arrive(2)
    for x in (1, layers - 2):
        advance(FOREIGN, 0, x)
    wait_halo(FOREIGN, 1)
    both(functools.partial(advance, FOREIGN, 1))
    send_halo(FOREIGN, 2)
    wait_halo(OWN, 2)
    both(functools.partial(advance, OWN, 2))
    send_halo(OWN, 3)
    loop(1, layers - 1, functools.partial(advance, OWN, 3))

    arrive(3)
    for x in (2, layers - 3):
        advance(FOREIGN, 0, x)
    for x in (1, layers - 2):
        advance(FOREIGN, 1, x)
    wait_halo(FOREIGN, 2)
    both(functools.partial(advance, FOREIGN, 2))
    send_halo(FOREIGN, 3)
    psi_copies = psi_halo()
    for copy in psi_copies:
        copy.start()
        sent.append(copy)
    loop(3, layers - 3, functools.partial(advance, FOREIGN, 0))
    loop(2, layers - 2, functools.partial(advance, FOREIGN, 1))
    loop(1, layers - 1, functools.partial(advance, FOREIGN, 2))
    wait_halo(OWN, 3)
    both(functools.partial(advance, OWN, 3))

    weights = [delta * (0.5 if t in (0, NS) else 1.0) for t in range(NS + 1)]
    charged = [weights[t] * q[t] for t in range(NS + 1)]

    def gathered(x):
        phi_layer, rho_layer = 0.0, 0.0
        for t in range(1, NS + 1):
            product = rounded[OWN, t, x] * rounded[FOREIGN, NS - t, x]
            phi_layer = phi_layer + weights[t] * product
            rho_layer = rho_layer + charged[t] * product
        return phi_layer, rho_layer

    def gather(x):
        phi[x], rho[x + 1] = gathered(x)

    def last_product(x):
        value = advanced(FOREIGN, NS - 1, x).astype(jnp.bfloat16).astype(jnp.float32)
        return rounded[OWN, 0, x] * value

    def finish(x):
        product = last_product(x)
        phi[x] += weights[0] * product
        rho[x + 1] += charged[0] * product

    def whole(x):
        phi_layer, rho_layer = gathered(x)
        product = last_product(x)
        phi[x] = phi_layer + weights[0] * product
        rho[x + 1] = rho_layer + charged[0] * product

    both(gather)
    loop(1, layers - 1, whole)

    inner = pl.ds(PAD, half)

    def add(x, carry):
        return carry + phi[x, inner]

    partial = lax.fori_loop(2, layers - 1, add, phi[1, inner])
    wait_halo(FOREIGN, NS - 1)
    both(finish)
    rho_copies = (
        pltpu.make_async_remote_copy(
            rho.at[1, inner], rho.at[layers + 1, inner], rho_send.at[0], rho_recv.at[0],
            device_id=left, device_id_type=MESH,
        ),
        pltpu.make_async_remote_copy(
            rho.at[layers, inner], rho.at[0, inner], rho_send.at[1], rho_recv.at[1],
            device_id=right, device_id_type=MESH,
        ),
    )
    partial = partial + phi[0, inner] + phi[layers - 1, inner]
    sums[0] = jnp.sum(
        sum(partial[:, k:k + 128] for k in range(0, partial.shape[1], 128)), axis=0, keepdims=True
    )

    def share(step, carry):
        pltpu.make_async_remote_copy(
            sums.at[0], sums.at[step], sum_send, sum_recv,
            device_id=device(step), device_id_type=MESH,
        ).start()
        return carry

    pl.semaphore_wait(gate.at[stages - 1], 1)
    lax.fori_loop(1, devices, share, 0)
    for copy in rho_copies:
        copy.start()
        sent.append(copy)

    for copy in psi_copies:
        copy.wait_recv()

    for x in (0, 1, layers, layers + 1):
        make_base(x)

    others = sums.at[pl.ds(1, devices - 1)]
    pltpu.make_async_copy(others, others, sum_recv).wait()
    cells = float(devices * layers * half * w_hbm.shape[2])
    inverse = cells / jnp.sum(sums[...])

    def relax_once(x):
        relaxed[x] = (base[x] + rho[x] * inverse) * (1.0 / (6.0 + screening))

    def first(x):
        density_ref[x] = phi[x, inner] * inverse
        relax_once(x + 1)

    loop(0, layers, first)

    def second(x):
        center = relaxed[x + 1]
        total = relaxed[x] + relaxed[x + 2] + around(center, 0) + around(center, 1)
        value = total + rho[x + 1] * inverse - ion_charge(center) + screening * center
        potential_ref[x] = value[PAD:PAD + half] * (1.0 / (6.0 + screening))

    loop(1, layers - 1, second)
    for copy in rho_copies:
        copy.wait_recv()
    relax_once(0)
    relax_once(layers + 1)
    both(second)

    for copy in sent:
        copy.wait_send()
    pltpu.make_async_copy(others, others, sum_send).wait()


def ion_charge(value):
    return (2.0 * screening) * jnp.tanh(0.5 * value)


def body(ends, slabs, w_field, psi_init, start_field, charges):
    layers, rows, depth = w_field.shape
    half = rows // ends
    wide = half + 2 * PAD
    devices = ends * slabs
    stages = slabs.bit_length()
    out = jax.ShapeDtypeStruct((layers, half, depth), jnp.float32)
    dma = pltpu.SemaphoreType.DMA

    def tile(*lead):
        return pltpu.VMEM((*lead, wide, depth), jnp.float32)

    hbm = pl.BlockSpec(memory_space=pltpu.HBM)
    vmem = pl.BlockSpec(memory_space=pltpu.VMEM)
    return pl.pallas_call(
        functools.partial(kernel, ends, slabs),
        out_shape=(out, out),
        in_specs=[pl.BlockSpec(memory_space=pltpu.SMEM), hbm, hbm, hbm],
        out_specs=(vmem, vmem),
        scratch_shapes=[
            tile(layers), tile(layers + 4), tile(2, layers), tile(NS, layers),
            tile(2, NS, layers + 2), tile(2, NS + 1, layers), tile(layers), tile(layers + 2),
            tile(layers + 2), tile(layers + 2), pltpu.VMEM((devices, 1, 128), jnp.float32),
            pltpu.SemaphoreType.REGULAR((stages,)), dma((3, 3)), dma((layers, 3)), dma((layers, 3)), dma((2, 3)), dma((2, 3)),
            dma((2, NS, 2)), dma((2, NS, 2)), dma((2,)), dma((2,)), dma(()), dma(()),
        ],
        compiler_params=pltpu.CompilerParams(
            collective_id=0, has_side_effects=True, vmem_limit_bytes=30 * 1024 * 1024
        ),
        name="scf_step",
    )(charges, *[pltpu.with_memory_space_constraint(v, pltpu.HBM) for v in (w_field, psi_init, start_field)])


def solution(mesh):
    in_specs = (P("slab", None, None), P("slab", None, None), P("end", "slab", None, None), P())
    out_specs = (P("slab", "end", None), P("slab", "end", None))
    step = functools.partial(body, mesh.shape["end"], mesh.shape["slab"])
    return jax.shard_map(step, mesh=mesh, in_specs=in_specs, out_specs=out_specs, check_vma=False)
```
